32 devices in a mesh: dp: 32 (over z, y, x, core).
Axes of the slice: x: 2, y: 2, z: 4, core: 2. Of those that a mesh axis runs over, the one named last changes fastest.
Arguments:
- patches: bfloat16 [32768, 1664], P('dp')
- ln_gain: float32 [1664], replicated, may hold values from 0.25 to 1.75
- w_qkv: bfloat16 [1664, 2496], P('dp')
- w_out: bfloat16 [832, 1664], P(None, 'dp'), may hold values from -0.21875 to 0.21875
- w_proj: bfloat16 [6656, 2048], P('dp'), may hold values from -0.078125 to 0.078125
- seg_ids: int32 [32768], P('dp'), may hold values from 0 to 4, as said below
- patch_mask: int32 [32768], P('dp'), may hold values 0 or 1
- grid_hw: int32 [128, 2], P('dp'), may hold values from 12 to 16, as said below
- owners: int32 [128], P('dp'), may hold values from 0 to 31
Outputs:
- routed: bfloat16 [8192, 2048], P('dp')
- image_rms: float32 [128], P('dp')
- image_max_logit: float32 [128], P('dp')
The draws below stay inside these ranges and needn't reach their ends.
Inputs may be any that keep to these rules, and one draw needn't show every extreme that they name: `seg_ids`: within each pack the images' tokens lie in order without gaps from the pack's first token, each image taking grid height times width consecutive tokens with segment numbers 0 to 3; the remaining tokens carry 4. `grid_hw`: heights and widths are 12, 14 or 16; every pack has an image of 16 x 16 patches, so an image has at most 64 merged rows, and every pack also has an image of height 12.
All inputs are finite; a program needn't handle non-finite values. No bound on the sum of `patch_mask` on one device may be relied on, other than what follows from the above.
Results may differ from the reference program's by a relative error of at most 0.006.
Values may be sent and summed in bfloat16 or wider, within the bound.
A program may use at most 192 MiB of HBM per device.

```python
import jax
import jax.numpy as jnp
from jax import lax

D = 1664
HEADS = 8
HEAD_DIM = 104
PROJ = 2048
TOK_DEV = 1024
CAP = 64
HW = 832
REQ_DEV = 4
WRAPS = 2
TOKENS = 32768
REQS = 128
N_DP = 32


def draw_patches(key, part):
    first_key = jax.random.fold_in(key, 0)
    values = jax.random.normal(first_key, (TOKENS, D), jnp.float32)
    return jnp.clip(values, -6.0, 6.0).astype(jnp.bfloat16)


def draw_w_qkv(key, part):
    hidden_w = HEADS * HEAD_DIM
    first_key = jax.random.fold_in(key, 0)
    base = jax.random.normal(first_key, (D, 3 * hidden_w), jnp.float32) * D ** (-0.5)
    return base.astype(jnp.bfloat16)


def image_layout(key):
    packs = REQS // REQ_DEV
    keys_all = jax.random.split(key, 3)
    side_h = 12 + 2 * jax.random.randint(keys_all[0], (packs, REQ_DEV), 0, 3)
    side_w = 12 + 2 * jax.random.randint(keys_all[1], (packs, REQ_DEV), 0, 3)
    biggest = jax.random.randint(keys_all[2], (packs, 1), 0, REQ_DEV)
    image_idx = jnp.arange(REQ_DEV, dtype=jnp.int32)[None, :]
    forced = image_idx == biggest
    shorter = image_idx == (biggest + 1) % REQ_DEV
    heights = jnp.where(forced, 16, jnp.where(shorter, 12, side_h)).astype(jnp.int32)
    widths = jnp.where(forced, 16, side_w).astype(jnp.int32)
    return (heights, widths)


def draw_grid_hw(key, part):
    heights, widths = image_layout(jax.random.fold_in(key, 11))
    return jnp.stack([heights, widths], axis=-1).reshape(REQS, 2).astype(jnp.int32)


def draw_seg_ids(key, part):
    heights, widths = image_layout(jax.random.fold_in(key, 11))
    areas = (heights * widths).astype(jnp.int32)
    ends_at = jnp.cumsum(areas, axis=1).astype(jnp.int32)
    position = jnp.arange(TOK_DEV, dtype=jnp.int32)
    seg_vals = jnp.sum((position[None, :, None] >= ends_at[:, None, :]).astype(jnp.int32), axis=2)
    return seg_vals.reshape(TOKENS).astype(jnp.int32)


def with_ends(drawn, stream_key, least, top_value):
    longest = drawn.shape.index(max(drawn.shape))
    spots = []
    for shift in (0, 1):
        where = [jax.random.randint(jax.random.fold_in(stream_key, axis), (), 0, length) for axis, length in enumerate(drawn.shape)]
        where[longest] = (where[longest] + shift) % drawn.shape[longest]
        spots.append(tuple(where))
    return drawn.at[spots[0]].set(least).at[spots[1]].set(top_value)


def level_of(rng, extent, cuts, least, largest):
    def one(axis_at, parts):
        steps = jax.random.uniform(jax.random.fold_in(jax.random.fold_in(rng, 6), axis_at), (parts,), jnp.float32, least / len(cuts), largest / len(cuts))
        return jnp.repeat(jnp.exp(steps), extent[axis_at] // parts).reshape((-1,) + (1,) * (len(extent) - axis_at - 1))

    factor_of = one(*cuts[0])
    for cut in cuts[1:]:
        factor_of = factor_of * one(*cut)
    return factor_of


def scatter_about(stream_key, shape, deviation, reach, cuts=(), kind=jnp.bfloat16):
    values = jax.random.normal(stream_key, shape, jnp.float32) * deviation
    if len(cuts) > 0:
        values = level_of(stream_key, shape, cuts, -0.22, 0.18) * values
    return jnp.clip(values, min=-reach, max=reach).astype(kind)


def setup_inputs(seed: int = 0) -> dict:
    key_list = jax.random.split(jax.random.key(seed), 10)
    patches = draw_patches(jax.random.fold_in(key_list[9], 71), 0)
    ln_gain = jnp.clip(1.0 + 0.15 * jax.random.normal(key_list[1], (D,), jnp.float32), 0.25, 1.75)
    w_qkv = draw_w_qkv(jax.random.fold_in(key_list[9], 71), 0)
    w_out = scatter_about(key_list[3], (HW, D), HW ** -0.5, 0.21875, ((1, 32),))
    w_proj = scatter_about(key_list[4], (4 * D, PROJ), (4 * D) ** -0.5, 0.078125, ((0, 32),))
    seg_ids = draw_seg_ids(jax.random.fold_in(key_list[9], 71), 0)
    patch_mask = with_ends((jax.random.randint(key_list[6], (TOKENS,), 0, 8) < 7).astype(jnp.int32), jax.random.fold_in(key_list[6], 1), 0, 1)
    grid_hw = draw_grid_hw(jax.random.fold_in(key_list[9], 71), 0)
    owners = with_ends(jax.random.randint(key_list[8], (REQS,), 0, N_DP), jax.random.fold_in(key_list[8], 1), 0, N_DP - 1).astype(jnp.int32)
    return {"patches": patches, "ln_gain": ln_gain, "w_qkv": w_qkv, "w_out": w_out, "w_proj": w_proj, "seg_ids": seg_ids, "patch_mask": patch_mask, "grid_hw": grid_hw, "owners": owners}


def token_places(seg_row, grid_rows):
    heights = grid_rows[:, 0]
    widths = grid_rows[:, 1]
    areas = (heights * widths).astype(jnp.int32)
    ends_at = jnp.cumsum(areas).astype(jnp.int32)
    starts = (ends_at - areas).astype(jnp.int32)
    image_count = grid_rows.shape[0]
    member = seg_row[:, None] == jnp.arange(image_count, dtype=jnp.int32)[None, :]
    start_tok = lax.optimization_barrier(jnp.sum(jnp.where(member, starts[None, :], 0), axis=1)).astype(jnp.int32)
    half_w = jnp.maximum(lax.optimization_barrier(jnp.sum(jnp.where(member, (widths // 2)[None, :], 0), axis=1)), 1).astype(jnp.int32)
    offset = jnp.arange(seg_row.shape[0], dtype=jnp.int32) - start_tok
    window = offset // 4
    corner = offset % 4
    row_pos = 2 * (window // half_w) + corner // 2
    col_pos = 2 * (window % half_w) + corner % 2
    return (row_pos.astype(jnp.float32), col_pos.astype(jnp.float32), areas, starts)

def rotate(heads_in, row_pos, col_pos):
    quarter = heads_in.shape[-1] // 4
    theta = 100.0 ** (-jnp.arange(quarter, dtype=jnp.float32) / quarter)
    out_parts = []
    for which_pos, offset_at in ((row_pos, 0), (col_pos, 2 * quarter)):
        angles = (which_pos[:, None] * theta[None, :])[:, None, :]
        cosine = jnp.cos(angles)
        sine_val = jnp.sin(angles)
        part_a = heads_in[..., offset_at:offset_at + quarter]
        part_b = heads_in[..., offset_at + quarter:offset_at + 2 * quarter]
        out_parts += [part_a * cosine - part_b * sine_val, part_a * sine_val + part_b * cosine]
    return jnp.concatenate(out_parts, axis=-1)

def send_rows(proj_bf, starts, areas, owner_row, device_count):
    merged_rows = proj_bf.shape[0]
    wrap_count = (CAP + device_count - 1) // device_count
    dest_ids = jnp.arange(device_count, dtype=jnp.int32)[:, None, None]
    wrap_ids = jnp.arange(wrap_count, dtype=jnp.int32)[None, None, :]
    owner_here = owner_row.astype(jnp.int32)[None, :, None]
    row_within = (wrap_ids * device_count + (dest_ids - owner_here) % device_count).astype(jnp.int32)
    row_total = (areas // 4).astype(jnp.int32)[None, :, None]
    first_row = (starts // 4).astype(jnp.int32)[None, :, None]
    picked = jnp.where(row_within < row_total, first_row + row_within, merged_rows).astype(jnp.int32)
    padded = jnp.concatenate([proj_bf, jnp.zeros((1, proj_bf.shape[1]), proj_bf.dtype)], axis=0)
    return padded[picked]

def attend(queries, key_rows, values, seg_query, seg_key, mask_key):
    scores = jnp.einsum('qhd,khd->hqk', queries.astype(jnp.float32), key_rows.astype(jnp.float32)) * queries.shape[-1] ** (-0.5)
    query_idx = jnp.arange(queries.shape[0], dtype=jnp.int32)
    key_idx = jnp.arange(key_rows.shape[0], dtype=jnp.int32)
    allowed = (seg_query[:, None] == seg_key[None, :]) & ((mask_key[None, :] == 1) | (query_idx[:, None] == key_idx[None, :]))
    masked = jnp.where(allowed[None], scores, -1e+30)
    top_row = lax.optimization_barrier(jnp.max(masked, axis=-1, keepdims=True))
    expo = jnp.where(allowed[None], jnp.exp(masked - top_row), 0.0)
    weights = (expo / lax.optimization_barrier(jnp.sum(expo, axis=-1, keepdims=True))).astype(jnp.bfloat16)
    result = jnp.einsum('hqk,khd->qhd', weights.astype(jnp.float32), values.astype(jnp.float32)).astype(jnp.bfloat16)
    return (result.reshape(queries.shape[0], -1), lax.optimization_barrier(jnp.max(top_row[..., 0], axis=0)))

def reference(patches, ln_gain, w_qkv, w_out, w_proj, seg_ids, patch_mask, grid_hw, owners):
    packs = N_DP
    hidden_w = HEADS * HEAD_DIM

    def one_pack(inputs):
        tokens_in, seg_row, mask_row, grid_rows, owner_row = inputs
        tokens_f = tokens_in.astype(jnp.float32)
        mean_row = lax.optimization_barrier(jnp.mean(tokens_f, axis=-1, keepdims=True))
        centered = tokens_f - mean_row
        var_row = lax.optimization_barrier(jnp.mean(centered * centered, axis=-1, keepdims=True))
        normed = (centered * lax.rsqrt(var_row + 1e-06) * ln_gain).astype(jnp.bfloat16)
        mixed = jnp.dot(normed, w_qkv, preferred_element_type=jnp.float32)
        row_pos, col_pos, areas, starts = token_places(seg_row, grid_rows)
        shape_three = (TOK_DEV, HEADS, HEAD_DIM)
        queries = rotate(mixed[:, :hidden_w].reshape(shape_three), row_pos, col_pos).astype(jnp.bfloat16)
        key_rows = rotate(mixed[:, hidden_w:2 * hidden_w].reshape(shape_three), row_pos, col_pos).astype(jnp.bfloat16)
        values = mixed[:, 2 * hidden_w:].reshape(shape_three).astype(jnp.bfloat16)
        attended, row_top = attend(queries, key_rows, values, seg_row, seg_row, mask_row)
        member_q = seg_row[:, None] == jnp.arange(REQ_DEV, dtype=jnp.int32)[None, :]
        top_logit = lax.optimization_barrier(jnp.max(jnp.where(member_q, row_top[:, None], -1e+30), axis=0))
        residual = (tokens_f + jnp.dot(attended, w_out, preferred_element_type=jnp.float32)).astype(jnp.bfloat16)
        merged = residual.reshape(TOK_DEV // 4, 4 * D)
        projected = jnp.dot(merged, w_proj, preferred_element_type=jnp.float32)
        proj_bf = projected.astype(jnp.bfloat16)
        merged_seg = seg_row.reshape(-1, 4)[:, 0]
        member_m = merged_seg[:, None] == jnp.arange(REQ_DEV, dtype=jnp.int32)[None, :]
        squares = lax.optimization_barrier(jnp.sum(projected * projected, axis=1))
        totals = lax.optimization_barrier(jnp.sum(jnp.where(member_m, squares[:, None], 0.0), axis=0))
        image_rms = jnp.sqrt(totals / (areas // 4 * PROJ).astype(jnp.float32))
        sent = send_rows(proj_bf, starts, areas, owner_row, packs)
        return (sent, image_rms, top_logit)
    sent, image_rms, top_logit = lax.map(one_pack, (patches.reshape(packs, TOK_DEV, D), seg_ids.reshape(packs, TOK_DEV), patch_mask.reshape(packs, TOK_DEV), grid_hw.reshape(packs, REQ_DEV, 2), owners.reshape(packs, REQ_DEV)))
    routed = jnp.transpose(sent, (1, 0, 2, 3, 4)).reshape(packs * packs * REQ_DEV * WRAPS, PROJ)
    return (routed, image_rms.reshape(REQS), top_logit.reshape(REQS))
```

```python
import functools

import jax
import jax.numpy as jnp
from jax import lax
from jax.experimental import pallas as pl
from jax.experimental.pallas import tpu as pltpu
from jax.sharding import PartitionSpec as P

HEADS = 8
CAP = 64
LANES = 128
MESH = pl.DeviceIdType.MESH


def token_places(seg_row, grid_rows):
    heights = grid_rows[:, 0]
    widths = grid_rows[:, 1]
    areas = heights * widths
    ends_at = jnp.cumsum(areas)
    starts = ends_at - areas
    image_count = grid_rows.shape[0]
    member = seg_row[:, None] == jnp.arange(image_count, dtype=jnp.int32)[None, :]
    start_tok = jnp.sum(jnp.where(member, starts[None, :], 0), axis=1)
    half_w = jnp.maximum(jnp.sum(jnp.where(member, (widths // 2)[None, :], 0), axis=1), 1)
    offset = jnp.arange(seg_row.shape[0], dtype=jnp.int32) - start_tok
    window = offset // 4
    corner = offset % 4
    row_pos = 2 * (window // half_w) + corner // 2
    col_pos = 2 * (window % half_w) + corner % 2
    return (row_pos.astype(jnp.float32), col_pos.astype(jnp.float32), areas, starts)


def rope_tables(row_pos, col_pos, head_dim):
    quarter = head_dim // 4
    lane = jnp.arange(LANES, dtype=jnp.int32)
    theta = 100.0 ** (-(lane % quarter).astype(jnp.float32) / quarter)
    part = lane // quarter
    pos = jnp.where(part[None, :] < 2, row_pos[:, None], col_pos[:, None])
    angles = pos * theta[None, :]
    cosine = jnp.cos(angles)
    sine = jnp.sin(angles)
    first = (part == 0) | (part == 2)
    second = (part == 1) | (part == 3)
    return (
        cosine,
        jnp.where(first[None, :], -sine, 0.0),
        jnp.where(second[None, :], sine, 0.0),
    )


def send_rows(proj_bf, starts, areas, owner_row, device_count):
    merged_rows = proj_bf.shape[0]
    wrap_count = (CAP + device_count - 1) // device_count
    dest_ids = jnp.arange(device_count, dtype=jnp.int32)[:, None, None]
    wrap_ids = jnp.arange(wrap_count, dtype=jnp.int32)[None, None, :]
    owner_here = owner_row[None, :, None]
    row_within = wrap_ids * device_count + (dest_ids - owner_here) % device_count
    row_total = (areas // 4)[None, :, None]
    first_row = (starts // 4)[None, :, None]
    picked = jnp.where(row_within < row_total, first_row + row_within, merged_rows)
    padded = jnp.concatenate([proj_bf, jnp.zeros((1, proj_bf.shape[1]), proj_bf.dtype)], axis=0)
    return padded[picked]


class Place:
    def __init__(self):
        me = lax.axis_index("dp")
        self.core = me % 2
        self.x = (me // 2) % 2
        self.y = (me // 4) % 2
        self.z = me // 8

    def line(self, r):
        z = self.z
        return (z, z + 1 - 2 * (z % 2), z + 2 - 4 * (z // 2), 3 - z)[r]

    def column(self, r, s):
        odd = (self.z + r) % 2
        x, y = self.x, self.y
        if s == 0:
            return y, x
        if s == 1:
            return y + odd * (1 - 2 * y), x + (1 - odd) * (1 - 2 * x)
        if s == 2:
            return y + (1 - odd) * (1 - 2 * y), x + odd * (1 - 2 * x)
        return 1 - y, 1 - x

    def chip(self, r, s):
        y, x = self.column(r, s)
        return (self.line(r) * 2 + y) * 2 + x

    def line_peer(self, r):
        return ((self.line(r) * 2 + self.y) * 2 + self.x) * 2 + self.core

    def side_peer(self, r, s):
        y, x = self.column(r, s)
        return ((self.z * 2 + y) * 2 + x) * 2 + self.core

    def twin(self):
        return ((self.z * 2 + self.y) * 2 + self.x) * 2 + 1 - self.core

    def greet(self):
        barrier = pltpu.get_barrier_semaphore()
        peers = [self.line_peer(r) for r in (1, 2, 3)]
        peers += [self.side_peer(0, 1), self.side_peer(0, 2), self.twin()]
        for peer in peers:
            pl.semaphore_signal(barrier, inc=1, device_id=(peer,), device_id_type=MESH)
        pl.semaphore_wait(barrier, len(peers))


class Gather:
    def __init__(self, place, src, dst_of, sems, at):
        self.place, self.src, self.dst_of = place, src, dst_of
        self.send, self.recv, self.twin_send, self.twin_recv, self.local = sems
        self.at = at
        self.ici = {}
        self.started = []

    def dst(self, r, s):
        return self.dst_of(self.place.chip(r, s))

    def remote(self, src, dst, send_sem, recv_sem, peer):
        copy = pltpu.make_async_remote_copy(
            src_ref=src,
            dst_ref=dst,
            send_sem=send_sem,
            recv_sem=recv_sem,
            device_id=(peer,),
            device_id_type=MESH,
        )
        copy.start()
        self.started.append(copy)
        return copy

    def over_links(self, src, unit, arrives, peer):
        n = self.at * 16 + arrives[0] * 4 + arrives[1]
        self.ici[arrives] = self.remote(
            src, self.dst(*unit), self.send.at[n], self.recv.at[n], peer
        )

    def to_twin(self, src, r, s):
        n = self.at * 16 + r * 4 + s
        self.twins.append(
            self.remote(
                src,
                self.dst(r, s),
                self.twin_send.at[n],
                self.twin_recv.at[n],
                self.place.twin(),
            )
        )

    def start(self):
        self.twins = []
        for r in (1, 2, 3):
            self.over_links(self.src, (0, 0), (r, 0), self.place.line_peer(r))
        self.spread(0)
        self.own = pltpu.make_async_copy(self.src, self.dst(0, 0), self.local.at[self.at])
        self.own.start()

    def spread(self, r):
        src = self.src if r == 0 else self.dst(r, 0)
        self.over_links(src, (r, 0), (r, 1), self.place.side_peer(r, 1))
        self.over_links(src, (r, 0), (r, 2), self.place.side_peer(r, 2))
        self.to_twin(src, r, 0)

    def second(self):
        for r in (1, 2, 3):
            self.ici[(r, 0)].wait_recv()
            self.spread(r)

    def third(self):
        for r in range(4):
            self.ici[(r, 1)].wait_recv()
            src = self.dst(r, 1)
            self.over_links(src, (r, 1), (r, 3), self.place.side_peer(r, 2))
            self.to_twin(src, r, 1)

    def fourth(self):
        for s in (2, 3):
            for r in range(4):
                self.ici[(r, s)].wait_recv()
                self.to_twin(self.dst(r, s), r, s)

    def finish(self):
        for copy in self.twins:
            copy.wait_recv()
        for copy in self.started:
            copy.wait_send()
        self.own.wait()


def gather_sems(chunks):
    return [pltpu.SemaphoreType.DMA((chunks * 16,))] * 4 + [pltpu.SemaphoreType.DMA((chunks,))]


def run_gathers(gathers, work):
    count = len(gathers)
    for step in range(count + 4):
        if step < count:
            gathers[step].start()
        work(step)
        if 0 <= step - 1 < count:
            gathers[step - 1].second()
        if 0 <= step - 2 < count:
            gathers[step - 2].third()
        if 0 <= step - 3 < count:
            gathers[step - 3].fourth()
        if 0 <= step - 4 < count:
            gathers[step - 4].finish()


def qkv_kernel(chunks, src_ref, out_ref, *sems):
    place = Place()
    place.greet()
    wide = src_ref.shape[1] // chunks
    gathers = []
    for q in range(chunks):
        cols = slice(q * wide, (q + 1) * wide)

        def dst_of(chip, cols=cols):
            return out_ref.at[place.core, chip, :, cols]

        gathers.append(Gather(place, src_ref.at[:, cols], dst_of, sems, q))
    run_gathers(gathers, lambda step: None)


def gather_qkv(block):
    rows, cols = block.shape
    chunks = 4
    return pl.pallas_call(
        functools.partial(qkv_kernel, chunks),
        out_shape=jax.ShapeDtypeStruct((2, 16, rows, cols), block.dtype),
        in_specs=[pl.BlockSpec(memory_space=pl.ANY)],
        out_specs=pl.BlockSpec(memory_space=pl.ANY),
        scratch_shapes=gather_sems(chunks),
        compiler_params=pltpu.CompilerParams(collective_id=0, has_side_effects=True),
    )(block)


def attend_kernel(
    chunks,
    scale,
    mixed_ref,
    cos_ref,
    sin_a_ref,
    sin_b_ref,
    seg_col_ref,
    seg_row_ref,
    mask_row_ref,
    wo_ref,
    wp_ref,
    att_ref,
    top_ref,
    wo_all,
    wp_all,
    q_buf,
    k_buf,
    v_buf,
    *sems,
):
    place = Place()
    place.greet()
    wide = wp_ref.shape[1] // chunks
    gathers = [
        Gather(place, wo_ref, lambda chip: wo_all.at[place.core, chip], sems, 0)
    ]
    for q in range(chunks):
        cols = slice(q * wide, (q + 1) * wide)

        def dst_of(chip, cols=cols):
            return wp_all.at[chip, place.core, :, cols]

        gathers.append(Gather(place, wp_ref.at[:, cols], dst_of, sems, q + 1))
    tokens = seg_col_ref.shape[0]
    block = 256
    half = HEADS // 2

    def turn(i, carry):
        rows = pl.ds(pl.multiple_of(i * block, block), block)
        cosine, sin_a, sin_b = cos_ref[rows, :], sin_a_ref[rows, :], sin_b_ref[rows, :]
        quarter = 26
        for h in range(HEADS):
            at = (h % half) * LANES
            out = slice(h * LANES, (h + 1) * LANES)
            for kind, buf in ((0, q_buf), (1, k_buf)):
                lanes = slice(kind * half * LANES + at, kind * half * LANES + at + LANES)
                val = mixed_ref[h // half, rows, lanes]
                turned = (
                    val * cosine
                    + pltpu.roll(val, LANES - quarter, 1) * sin_a
                    + pltpu.roll(val, quarter, 1) * sin_b
                )
                buf[rows, out] = turned.astype(jnp.bfloat16)
            lanes = slice(2 * half * LANES + at, 2 * half * LANES + at + LANES)
            v_buf[rows, out] = mixed_ref[h // half, rows, lanes].astype(jnp.bfloat16)
        return carry

    def one_block(i, carry):
        rows = pl.ds(pl.multiple_of(i * block, block), block)
        seg_q = seg_col_ref[rows, :]
        query_idx = i * block + lax.broadcasted_iota(jnp.int32, (block, tokens), 0)
        key_idx = lax.broadcasted_iota(jnp.int32, (block, tokens), 1)
        allowed = (seg_q == seg_row_ref[...]) & (
            (mask_row_ref[...] == 1) | (query_idx == key_idx)
        )
        bias = jnp.where(allowed, 0.0, -1e30)
        best = jnp.full((block, 1), -1e30, jnp.float32)
        for h in range(HEADS):
            lanes = slice(h * LANES, (h + 1) * LANES)
            scores = lax.dot_general(
                q_buf[rows, lanes],
                k_buf[:, lanes],
                (((1,), (1,)), ((), ())),
                preferred_element_type=jnp.float32,
            )
            scores = scores * scale + bias
            top = jnp.max(scores, axis=1, keepdims=True)
            best = jnp.maximum(best, top)
            expo = jnp.exp(scores - top)
            total = jnp.sum(expo, axis=1, keepdims=True)
            got = jnp.dot(
                expo.astype(jnp.bfloat16), v_buf[:, lanes], preferred_element_type=jnp.float32
            )
            att_ref[rows, lanes] = (got / total).astype(jnp.bfloat16)
        top_ref[rows, :] = jnp.broadcast_to(best, (block, LANES))
        return carry

    blocks = tokens // block

    def work(step):
        if step == 0:
            lax.fori_loop(0, blocks, turn, 0)
        elif step == 1:
            lax.fori_loop(0, blocks // 2, one_block, 0)
        elif step == 2:
            lax.fori_loop(blocks // 2, blocks, one_block, 0)

    run_gathers(gathers, work)


def attend_and_gather(mixed, tables, seg, mask, wo_block, w_proj, head_dim):
    tokens = seg.shape[0]
    chunks = 4
    wide = HEADS * LANES
    vmem = pl.BlockSpec(memory_space=pltpu.VMEM)
    hbm = pl.BlockSpec(memory_space=pl.ANY)
    return pl.pallas_call(
        functools.partial(attend_kernel, chunks, head_dim ** (-0.5)),
        out_shape=(
            jax.ShapeDtypeStruct((tokens, wide), jnp.bfloat16),
            jax.ShapeDtypeStruct((tokens, LANES), jnp.float32),
            jax.ShapeDtypeStruct((2, 16) + wo_block.shape, jnp.bfloat16),
            jax.ShapeDtypeStruct((16, 2) + w_proj.shape, jnp.bfloat16),
        ),
        in_specs=[vmem] * 7 + [hbm] * 2,
        out_specs=(vmem, vmem, hbm, hbm),
        scratch_shapes=[pltpu.VMEM((tokens, wide), jnp.bfloat16)] * 3 + gather_sems(chunks + 1),
        compiler_params=pltpu.CompilerParams(
            collective_id=1, has_side_effects=True, vmem_limit_bytes=48 * 1024 * 1024
        ),
    )(mixed, *tables, seg[:, None], seg[None, :], mask[None, :], wo_block, w_proj)


def pair_blocks(w_qkv, w_out, head_dim):
    core = lax.axis_index("dp") % 2
    rows = w_qkv.shape[0]
    half = HEADS // 2
    pad = LANES - head_dim
    mine = jnp.concatenate([w_qkv, w_out.T], axis=1)
    twin = [(i, i + 1 - 2 * (i % 2)) for i in range(lax.axis_size("dp"))]
    parts = mine.reshape(rows, 4, 2, half, head_dim)
    keep = jnp.where(core == 0, parts[:, :, 0], parts[:, :, 1])
    give = jnp.where(core == 0, parts[:, :, 1], parts[:, :, 0])
    got = lax.ppermute(give.reshape(rows, -1), "dp", twin).reshape(keep.shape)
    both = jnp.concatenate(
        [jnp.where(core == 0, keep, got), jnp.where(core == 0, got, keep)], axis=0
    )
    both = jnp.pad(both, ((0, 0), (0, 0), (0, 0), (0, pad))).reshape(2 * rows, 4, half * LANES)
    return both[:, :3].reshape(2 * rows, 3 * half * LANES), both[:, 3]


def plain_gathers(normed, tables, seg_ids, patch_mask, w_qkv, w_out, w_proj):
    tok_count = normed.shape[0]
    hidden_w = w_out.shape[0]
    head_dim = hidden_w // HEADS
    quarter = head_dim // 4
    mixed = jnp.dot(
        normed, lax.all_gather(w_qkv, "dp", axis=0, tiled=True), preferred_element_type=jnp.float32
    )
    shape_three = (tok_count, HEADS, head_dim)
    cosine, sin_a, sin_b = [t[:, None, :head_dim] for t in tables]

    def rotate(val):
        return (
            val * cosine
            + jnp.roll(val, -quarter, axis=2) * sin_a
            + jnp.roll(val, quarter, axis=2) * sin_b
        ).astype(jnp.bfloat16)

    queries = rotate(mixed[:, :hidden_w].reshape(shape_three))
    key_rows = rotate(mixed[:, hidden_w : 2 * hidden_w].reshape(shape_three))
    values = mixed[:, 2 * hidden_w :].reshape(shape_three).astype(jnp.bfloat16)
    scores = jnp.einsum("qhd,khd->hqk", queries, key_rows, preferred_element_type=jnp.float32)
    idx = jnp.arange(tok_count, dtype=jnp.int32)
    allowed = (seg_ids[:, None] == seg_ids[None, :]) & (
        (patch_mask[None, :] == 1) | (idx[:, None] == idx[None, :])
    )
    masked = jnp.where(allowed[None], scores * head_dim ** (-0.5), -1e30)
    weights = jax.nn.softmax(masked, axis=-1).astype(jnp.bfloat16)
    attended = jnp.einsum("hqk,khd->qhd", weights, values, preferred_element_type=jnp.float32)
    attended = attended.astype(jnp.bfloat16).reshape(tok_count, hidden_w)
    out_term = jnp.dot(
        attended,
        lax.all_gather(w_out, "dp", axis=1, tiled=True),
        preferred_element_type=jnp.float32,
    )
    return out_term, jnp.max(masked, axis=(0, 2)), lax.all_gather(w_proj, "dp", axis=0, tiled=True)


def chip_gathers(normed, tables, seg_ids, patch_mask, w_qkv, w_out, w_proj):
    head_dim = w_out.shape[0] // HEADS
    qkv_block, wo_block = pair_blocks(w_qkv, w_out, head_dim)
    wq = gather_qkv(qkv_block).reshape(2, -1, qkv_block.shape[1])
    mixed = jnp.stack(
        [jnp.dot(normed, wq[i], preferred_element_type=jnp.float32) for i in range(2)]
    )
    att, top, wo, wp = attend_and_gather(
        mixed, tables, seg_ids, patch_mask, wo_block, w_proj, head_dim
    )
    wo = wo.reshape(2, -1, wo_block.shape[1])
    span = wo.shape[2]
    dims = (((1,), (1,)), ((), ()))
    out_term = lax.dot_general(
        att[:, :span], wo[0], dims, preferred_element_type=jnp.float32
    ) + lax.dot_general(att[:, span:], wo[1], dims, preferred_element_type=jnp.float32)
    return out_term, top[:, 0], wp.reshape(-1, w_proj.shape[1])


def on_device(patches, ln_gain, w_qkv, w_out, w_proj, seg_ids, patch_mask, grid_hw, owners):
    tok_count, width_in = patches.shape
    head_dim = w_out.shape[0] // HEADS
    image_count = grid_hw.shape[0]
    proj_w = w_proj.shape[1]
    devices = lax.axis_size("dp")
    tokens_f = patches.astype(jnp.float32)
    mean_row = jnp.mean(tokens_f, axis=-1, keepdims=True)
    centered = tokens_f - mean_row
    var_row = jnp.mean(centered * centered, axis=-1, keepdims=True)
    normed = (centered * lax.rsqrt(var_row + 1e-06) * ln_gain).astype(jnp.bfloat16)
    row_pos, col_pos, areas, starts = token_places(seg_ids, grid_hw)
    tables = rope_tables(row_pos, col_pos, head_dim)
    image_ids = jnp.arange(image_count, dtype=jnp.int32)
    path = chip_gathers if devices == 32 else plain_gathers
    out_term, row_top, wp = path(normed, tables, seg_ids, patch_mask, w_qkv, w_out, w_proj)
    member_q = seg_ids[:, None] == image_ids[None, :]
    top_logit = jnp.max(jnp.where(member_q, row_top[:, None], -1e30), axis=0)
    residual = (tokens_f + out_term).astype(jnp.bfloat16)
    merged = residual.reshape(tok_count // 4, 4 * width_in)
    projected = jnp.dot(merged, wp, preferred_element_type=jnp.float32)
    proj_bf = projected.astype(jnp.bfloat16)
    merged_seg = seg_ids.reshape(-1, 4)[:, 0]
    member_m = merged_seg[:, None] == image_ids[None, :]
    squares = jnp.sum(projected * projected, axis=1)
    totals = jnp.sum(jnp.where(member_m, squares[:, None], 0.0), axis=0)
    image_rms = jnp.sqrt(totals / (areas // 4 * proj_w).astype(jnp.float32))
    sent = send_rows(proj_bf, starts, areas, owners, devices)
    arrived = lax.all_to_all(sent, "dp", split_axis=0, concat_axis=0, tiled=True)
    return (arrived.reshape(-1, proj_w), image_rms, top_logit)


def solution(mesh):
    return jax.shard_map(
        on_device,
        mesh=mesh,
        in_specs=(
            P("dp", None),
            P(),
            P("dp", None),
            P(None, "dp"),
            P("dp", None),
            P("dp"),
            P("dp"),
            P("dp", None),
            P("dp"),
        ),
        out_specs=(P("dp", None), P("dp"), P("dp")),
        check_vma=False,
    )
```

```python
import functools

import jax
import jax.numpy as jnp
from jax import lax
from jax.experimental import pallas as pl
from jax.experimental.pallas import tpu as pltpu
from jax.sharding import PartitionSpec as P

HEADS = 8
CAP = 64
LANES = 128
MESH = pl.DeviceIdType.MESH


def token_places(seg_row, grid_rows):
    heights = grid_rows[:, 0]
    widths = grid_rows[:, 1]
    areas = heights * widths
    ends_at = jnp.cumsum(areas)
    starts = ends_at - areas
    image_count = grid_rows.shape[0]
    member = seg_row[:, None] == jnp.arange(image_count, dtype=jnp.int32)[None, :]
    start_tok = jnp.sum(jnp.where(member, starts[None, :], 0), axis=1)
    half_w = jnp.maximum(jnp.sum(jnp.where(member, (widths // 2)[None, :], 0), axis=1), 1)
    offset = jnp.arange(seg_row.shape[0], dtype=jnp.int32) - start_tok
    window = offset // 4
    corner = offset % 4
    row_pos = 2 * (window // half_w) + corner // 2
    col_pos = 2 * (window % half_w) + corner % 2
    return (row_pos.astype(jnp.float32), col_pos.astype(jnp.float32), areas, starts)


def rope_tables(row_pos, col_pos, head_dim):
    quarter = head_dim // 4
    lane = jnp.arange(LANES, dtype=jnp.int32)
    theta = 100.0 ** (-(lane % quarter).astype(jnp.float32) / quarter)
    part = lane // quarter
    pos = jnp.where(part[None, :] < 2, row_pos[:, None], col_pos[:, None])
    angles = pos * theta[None, :]
    cosine = jnp.cos(angles)
    sine = jnp.sin(angles)
    first = (part == 0) | (part == 2)
    second = (part == 1) | (part == 3)
    return (
        cosine,
        jnp.where(first[None, :], -sine, 0.0),
        jnp.where(second[None, :], sine, 0.0),
    )


def send_rows(proj_bf, starts, areas, owner_row, device_count):
    merged_rows = proj_bf.shape[0]
    wrap_count = (CAP + device_count - 1) // device_count
    dest_ids = jnp.arange(device_count, dtype=jnp.int32)[:, None, None]
    wrap_ids = jnp.arange(wrap_count, dtype=jnp.int32)[None, None, :]
    owner_here = owner_row[None, :, None]
    row_within = wrap_ids * device_count + (dest_ids - owner_here) % device_count
    row_total = (areas // 4)[None, :, None]
    first_row = (starts // 4)[None, :, None]
    picked = jnp.where(row_within < row_total, first_row + row_within, merged_rows)
    padded = jnp.concatenate([proj_bf, jnp.zeros((1, proj_bf.shape[1]), proj_bf.dtype)], axis=0)
    return padded[picked]


class Place:
    def __init__(self):
        me = lax.axis_index("dp")
        self.core = me % 2
        self.x = (me // 2) % 2
        self.y = (me // 4) % 2
        self.z = me // 8

    def line(self, r):
        z = self.z
        return (z, z + 1 - 2 * (z % 2), z + 2 - 4 * (z // 2), 3 - z)[r]

    def column(self, r, s):
        odd = (self.z + r) % 2
        x, y = self.x, self.y
        if s == 0:
            return y, x
        if s == 1:
            return y + odd * (1 - 2 * y), x + (1 - odd) * (1 - 2 * x)
        if s == 2:
            return y + (1 - odd) * (1 - 2 * y), x + odd * (1 - 2 * x)
        return 1 - y, 1 - x

    def chip(self, r, s):
        y, x = self.column(r, s)
        return (self.line(r) * 2 + y) * 2 + x

    def line_peer(self, r):
        return ((self.line(r) * 2 + self.y) * 2 + self.x) * 2 + self.core

    def side_peer(self, r, s):
        y, x = self.column(r, s)
        return ((self.z * 2 + y) * 2 + x) * 2 + self.core

    def twin(self):
        return ((self.z * 2 + self.y) * 2 + self.x) * 2 + 1 - self.core

    def greet(self):
        barrier = pltpu.get_barrier_semaphore()
        peers = [self.line_peer(r) for r in (1, 2, 3)]
        peers += [self.side_peer(0, 1), self.side_peer(0, 2), self.twin()]
        for peer in peers:
            pl.semaphore_signal(barrier, inc=1, device_id=(peer,), device_id_type=MESH)
        pl.semaphore_wait(barrier, len(peers))


class Gather:
    def __init__(self, place, src, dst_of, sems, at):
        self.place, self.src, self.dst_of = place, src, dst_of
        self.send, self.recv, self.twin_send, self.twin_recv, self.local = sems
        self.at = at
        self.ici = {}
        self.started = []

    def dst(self, r, s):
        return self.dst_of(self.place.chip(r, s))

    def remote(self, src, dst, send_sem, recv_sem, peer):
        copy = pltpu.make_async_remote_copy(
            src_ref=src,
            dst_ref=dst,
            send_sem=send_sem,
            recv_sem=recv_sem,
            device_id=(peer,),
            device_id_type=MESH,
        )
        copy.start()
        self.started.append(copy)
        return copy

    def over_links(self, src, unit, arrives, peer):
        n = self.at * 16 + arrives[0] * 4 + arrives[1]
        self.ici[arrives] = self.remote(
            src, self.dst(*unit), self.send.at[n], self.recv.at[n], peer
        )

    def to_twin(self, src, r, s):
        n = self.at * 16 + r * 4 + s
        self.twins.append(
            self.remote(
                src,
                self.dst(r, s),
                self.twin_send.at[n],
                self.twin_recv.at[n],
                self.place.twin(),
            )
        )

    def start(self):
        self.twins = []
        for r in (1, 2, 3):
            self.over_links(self.src, (0, 0), (r, 0), self.place.line_peer(r))
        self.spread(0)
        self.own = pltpu.make_async_copy(self.src, self.dst(0, 0), self.local.at[self.at])
        self.own.start()

    def spread(self, r):
        src = self.src if r == 0 else self.dst(r, 0)
        self.over_links(src, (r, 0), (r, 1), self.place.side_peer(r, 1))
        self.over_links(src, (r, 0), (r, 2), self.place.side_peer(r, 2))
        self.to_twin(src, r, 0)

    def second(self):
        for r in (1, 2, 3):
            self.ici[(r, 0)].wait_recv()
            self.spread(r)

    def third(self):
        for r in range(4):
            self.ici[(r, 1)].wait_recv()
            src = self.dst(r, 1)
            self.over_links(src, (r, 1), (r, 3), self.place.side_peer(r, 2))
            self.to_twin(src, r, 1)

    def fourth(self):
        for s in (2, 3):
            for r in range(4):
                self.ici[(r, s)].wait_recv()
                self.to_twin(self.dst(r, s), r, s)

    def finish(self):
        for copy in self.twins:
            copy.wait_recv()
        for copy in self.started:
            copy.wait_send()
        self.own.wait()


def gather_sems(chunks):
    return [pltpu.SemaphoreType.DMA((chunks * 16,))] * 4 + [pltpu.SemaphoreType.DMA((chunks,))]


def run_gathers(gathers, work):
    count = len(gathers)
    for step in range(count + 4):
        if step < count:
            gathers[step].start()
        work(step)
        if 0 <= step - 1 < count:
            gathers[step - 1].second()
        if 0 <= step - 2 < count:
            gathers[step - 2].third()
        if 0 <= step - 3 < count:
            gathers[step - 3].fourth()
        if 0 <= step - 4 < count:
            gathers[step - 4].finish()


def attend_kernel(
    q_chunks,
    p_chunks,
    scale,
    patches_ref,
    gain_ref,
    cos_ref,
    sin_a_ref,
    sin_b_ref,
    seg_col_ref,
    seg_row_ref,
    mask_row_ref,
    wq_ref,
    wo_ref,
    wp_ref,
    att_ref,
    top_ref,
    wq_all,
    wo_all,
    wp_all,
    wq_buf,
    q_buf,
    k_buf,
    v_buf,
    load_sem,
    *sems,
):
    place = Place()
    place.greet()
    depth, wq_cols = wq_ref.shape
    gathers = []
    wide = wq_cols // q_chunks
    for q in range(q_chunks):
        cols = slice(q * wide, (q + 1) * wide)

        def dst_of(chip, cols=cols):
            rows = pl.ds(pl.multiple_of(chip * depth, 8), depth)
            return wq_all.at[place.core, rows, cols]

        gathers.append(Gather(place, wq_ref.at[:, cols], dst_of, sems, len(gathers)))
    gathers.append(
        Gather(place, wo_ref, lambda chip: wo_all.at[place.core, chip], sems, len(gathers))
    )
    wide = wp_ref.shape[1] // p_chunks
    for q in range(p_chunks):
        cols = slice(q * wide, (q + 1) * wide)

        def dst_of(chip, cols=cols):
            return wp_all.at[chip, place.core, :, cols]

        gathers.append(Gather(place, wp_ref.at[:, cols], dst_of, sems, len(gathers)))
    tokens, width = patches_ref.shape
    block = 256
    half = HEADS // 2
    quarter = 26

    def project(i, carry):
        rows = pl.ds(pl.multiple_of(i * block, block), block)
        tokens_f = patches_ref[rows, :].astype(jnp.float32)
        centered = tokens_f - jnp.mean(tokens_f, axis=1, keepdims=True)
        var = jnp.mean(centered * centered, axis=1, keepdims=True)
        normed = (centered * lax.rsqrt(var + 1e-06) * gain_ref[...]).astype(jnp.bfloat16)
        cosine, sin_a, sin_b = cos_ref[rows, :], sin_a_ref[rows, :], sin_b_ref[rows, :]
        for part in range(2):
            mixed = jnp.dot(normed, wq_buf[part], preferred_element_type=jnp.float32)
            for kind, buf in ((0, q_buf), (1, k_buf), (2, v_buf)):
                for h in range(half):
                    at = (kind * half + h) * LANES
                    val = mixed[:, at : at + LANES]
                    if kind < 2:
                        val = (
                            val * cosine
                            + pltpu.roll(val, LANES - quarter, 1) * sin_a
                            + pltpu.roll(val, quarter, 1) * sin_b
                        )
                    out = (part * half + h) * LANES
                    buf[rows, out : out + LANES] = val.astype(jnp.bfloat16)
        return carry

    def one_block(i, carry):
        rows = pl.ds(pl.multiple_of(i * block, block), block)
        seg_q = seg_col_ref[rows, :]
        query_idx = i * block + lax.broadcasted_iota(jnp.int32, (block, tokens), 0)
        key_idx = lax.broadcasted_iota(jnp.int32, (block, tokens), 1)
        allowed = (seg_q == seg_row_ref[...]) & (
            (mask_row_ref[...] == 1) | (query_idx == key_idx)
        )
        bias = jnp.where(allowed, 0.0, -1e30)
        best = jnp.full((block, 1), -1e30, jnp.float32)
        for h in range(HEADS):
            lanes = slice(h * LANES, (h + 1) * LANES)
            scores = lax.dot_general(
                q_buf[rows, lanes],
                k_buf[:, lanes],
                (((1,), (1,)), ((), ())),
                preferred_element_type=jnp.float32,
            )
            scores = scores * scale + bias
            top = jnp.max(scores, axis=1, keepdims=True)
            best = jnp.maximum(best, top)
            expo = jnp.exp(scores - top)
            total = jnp.sum(expo, axis=1, keepdims=True)
            got = jnp.dot(
                expo.astype(jnp.bfloat16), v_buf[:, lanes], preferred_element_type=jnp.float32
            )
            att_ref[rows, lanes] = (got / total).astype(jnp.bfloat16)
        top_ref[rows, :] = jnp.broadcast_to(best, (block, LANES))
        return carry

    blocks = tokens // block
    loaded = q_chunks + 4

    def work(step):
        if step == loaded:
            load = pltpu.make_async_copy(wq_all, wq_buf, load_sem)
            load.start()
            load.wait()
            lax.fori_loop(0, blocks // 2, project, 0)
        elif step == loaded + 1:
            lax.fori_loop(blocks // 2, blocks, project, 0)
        elif step == loaded + 2:
            lax.fori_loop(0, blocks // 2, one_block, 0)
        elif step == loaded + 3:
            lax.fori_loop(blocks // 2, blocks, one_block, 0)

    run_gathers(gathers, work)


def attend_and_gather(patches, gain, tables, seg, mask, wq_block, wo_block, w_proj, head_dim):
    tokens, width = patches.shape
    q_chunks, p_chunks = 4, 8
    wide = HEADS * LANES
    vmem = pl.BlockSpec(memory_space=pltpu.VMEM)
    hbm = pl.BlockSpec(memory_space=pl.ANY)
    wq_shape = (2, width, wq_block.shape[1])
    return pl.pallas_call(
        functools.partial(attend_kernel, q_chunks, p_chunks, head_dim ** (-0.5)),
        out_shape=(
            jax.ShapeDtypeStruct((tokens, wide), jnp.bfloat16),
            jax.ShapeDtypeStruct((tokens, LANES), jnp.float32),
            jax.ShapeDtypeStruct(wq_shape, jnp.bfloat16),
            jax.ShapeDtypeStruct((2, 16) + wo_block.shape, jnp.bfloat16),
            jax.ShapeDtypeStruct((16, 2) + w_proj.shape, jnp.bfloat16),
        ),
        in_specs=[vmem] * 8 + [hbm] * 3,
        out_specs=(vmem, vmem, hbm, hbm, hbm),
        scratch_shapes=[pltpu.VMEM(wq_shape, jnp.bfloat16)]
        + [pltpu.VMEM((tokens, wide), jnp.bfloat16)] * 3
        + [pltpu.SemaphoreType.DMA]
        + gather_sems(q_chunks + 1 + p_chunks),
        compiler_params=pltpu.CompilerParams(
            collective_id=1, has_side_effects=True, vmem_limit_bytes=56 * 1024 * 1024
        ),
    )(
        patches,
        gain[None, :],
        *tables,
        seg[:, None],
        seg[None, :],
        mask[None, :],
        wq_block,
        wo_block,
        w_proj,
    )


def pair_blocks(w_qkv, w_out, head_dim):
    core = lax.axis_index("dp") % 2
    rows = w_qkv.shape[0]
    half = HEADS // 2
    pad = LANES - head_dim
    mine = jnp.concatenate([w_qkv, w_out.T], axis=1)
    twin = [(i, i + 1 - 2 * (i % 2)) for i in range(lax.axis_size("dp"))]
    parts = mine.reshape(rows, 4, 2, half, head_dim)
    keep = jnp.where(core == 0, parts[:, :, 0], parts[:, :, 1])
    give = jnp.where(core == 0, parts[:, :, 1], parts[:, :, 0])
    got = lax.ppermute(give.reshape(rows, -1), "dp", twin).reshape(keep.shape)
    both = jnp.concatenate(
        [jnp.where(core == 0, keep, got), jnp.where(core == 0, got, keep)], axis=0
    )
    both = jnp.pad(both, ((0, 0), (0, 0), (0, 0), (0, pad))).reshape(2 * rows, 4, half * LANES)
    return both[:, :3].reshape(2 * rows, 3 * half * LANES), both[:, 3]


def plain_gathers(patches, ln_gain, tables, seg_ids, patch_mask, w_qkv, w_out, w_proj):
    tok_count = patches.shape[0]
    tokens_f = patches.astype(jnp.float32)
    mean_row = jnp.mean(tokens_f, axis=-1, keepdims=True)
    centered = tokens_f - mean_row
    var_row = jnp.mean(centered * centered, axis=-1, keepdims=True)
    normed = (centered * lax.rsqrt(var_row + 1e-06) * ln_gain).astype(jnp.bfloat16)
    hidden_w = w_out.shape[0]
    head_dim = hidden_w // HEADS
    quarter = head_dim // 4
    mixed = jnp.dot(
        normed, lax.all_gather(w_qkv, "dp", axis=0, tiled=True), preferred_element_type=jnp.float32
    )
    shape_three = (tok_count, HEADS, head_dim)
    cosine, sin_a, sin_b = [t[:, None, :head_dim] for t in tables]

    def rotate(val):
        return (
            val * cosine
            + jnp.roll(val, -quarter, axis=2) * sin_a
            + jnp.roll(val, quarter, axis=2) * sin_b
        ).astype(jnp.bfloat16)

    queries = rotate(mixed[:, :hidden_w].reshape(shape_three))
    key_rows = rotate(mixed[:, hidden_w : 2 * hidden_w].reshape(shape_three))
    values = mixed[:, 2 * hidden_w :].reshape(shape_three).astype(jnp.bfloat16)
    scores = jnp.einsum("qhd,khd->hqk", queries, key_rows, preferred_element_type=jnp.float32)
    idx = jnp.arange(tok_count, dtype=jnp.int32)
    allowed = (seg_ids[:, None] == seg_ids[None, :]) & (
        (patch_mask[None, :] == 1) | (idx[:, None] == idx[None, :])
    )
    masked = jnp.where(allowed[None], scores * head_dim ** (-0.5), -1e30)
    weights = jax.nn.softmax(masked, axis=-1).astype(jnp.bfloat16)
    attended = jnp.einsum("hqk,khd->qhd", weights, values, preferred_element_type=jnp.float32)
    attended = attended.astype(jnp.bfloat16).reshape(tok_count, hidden_w)
    out_term = jnp.dot(
        attended,
        lax.all_gather(w_out, "dp", axis=1, tiled=True),
        preferred_element_type=jnp.float32,
    )
    return out_term, jnp.max(masked, axis=(0, 2)), lax.all_gather(w_proj, "dp", axis=0, tiled=True)


def chip_gathers(patches, ln_gain, tables, seg_ids, patch_mask, w_qkv, w_out, w_proj):
    head_dim = w_out.shape[0] // HEADS
    wq_block, wo_block = pair_blocks(w_qkv, w_out, head_dim)
    att, top, _, wo, wp = attend_and_gather(
        patches, ln_gain, tables, seg_ids, patch_mask, wq_block, wo_block, w_proj, head_dim
    )
    wo = wo.reshape(2, -1, wo_block.shape[1])
    span = wo.shape[2]
    dims = (((1,), (1,)), ((), ()))
    out_term = lax.dot_general(
        att[:, :span], wo[0], dims, preferred_element_type=jnp.float32
    ) + lax.dot_general(att[:, span:], wo[1], dims, preferred_element_type=jnp.float32)
    return out_term, top[:, 0], wp.reshape(-1, w_proj.shape[1])


def on_device(patches, ln_gain, w_qkv, w_out, w_proj, seg_ids, patch_mask, grid_hw, owners):
    tok_count, width_in = patches.shape
    head_dim = w_out.shape[0] // HEADS
    image_count = grid_hw.shape[0]
    proj_w = w_proj.shape[1]
    devices = lax.axis_size("dp")
    tokens_f = patches.astype(jnp.float32)
    row_pos, col_pos, areas, starts = token_places(seg_ids, grid_hw)
    tables = rope_tables(row_pos, col_pos, head_dim)
    image_ids = jnp.arange(image_count, dtype=jnp.int32)
    path = chip_gathers if devices == 32 else plain_gathers
    out_term, row_top, wp = path(
        patches, ln_gain, tables, seg_ids, patch_mask, w_qkv, w_out, w_proj
    )
    member_q = seg_ids[:, None] == image_ids[None, :]
    top_logit = jnp.max(jnp.where(member_q, row_top[:, None], -1e30), axis=0)
    residual = (tokens_f + out_term).astype(jnp.bfloat16)
    merged = residual.reshape(tok_count // 4, 4 * width_in)
    projected = jnp.dot(merged, wp, preferred_element_type=jnp.float32)
    proj_bf = projected.astype(jnp.bfloat16)
    merged_seg = seg_ids.reshape(-1, 4)[:, 0]
    member_m = merged_seg[:, None] == image_ids[None, :]
    squares = jnp.sum(projected * projected, axis=1)
    totals = jnp.sum(jnp.where(member_m, squares[:, None], 0.0), axis=0)
    image_rms = jnp.sqrt(totals / (areas // 4 * proj_w).astype(jnp.float32))
    sent = send_rows(proj_bf, starts, areas, owners, devices)
    arrived = lax.all_to_all(sent, "dp", split_axis=0, concat_axis=0, tiled=True)
    return (arrived.reshape(-1, proj_w), image_rms, top_logit)


def solution(mesh):
    return jax.shard_map(
        on_device,
        mesh=mesh,
        in_specs=(
            P("dp", None),
            P(),
            P("dp", None),
            P(None, "dp"),
            P("dp", None),
            P("dp"),
            P("dp"),
            P("dp", None),
            P("dp"),
        ),
        out_specs=(P("dp", None), P("dp"), P("dp")),
        check_vma=False,
    )
```

```python
import functools

import jax
import jax.numpy as jnp
from jax import lax
from jax.experimental import pallas as pl
from jax.experimental.pallas import tpu as pltpu
from jax.sharding import PartitionSpec as P

HEADS = 8
CAP = 64
LANES = 128
MESH = pl.DeviceIdType.MESH


def token_places(seg_row, grid_rows):
    heights = grid_rows[:, 0]
    widths = grid_rows[:, 1]
    areas = heights * widths
    ends_at = jnp.cumsum(areas)
    starts = ends_at - areas
    image_count = grid_rows.shape[0]
    member = seg_row[:, None] == jnp.arange(image_count, dtype=jnp.int32)[None, :]
    start_tok = jnp.sum(jnp.where(member, starts[None, :], 0), axis=1)
    half_w = jnp.maximum(jnp.sum(jnp.where(member, (widths // 2)[None, :], 0), axis=1), 1)
    offset = jnp.arange(seg_row.shape[0], dtype=jnp.int32) - start_tok
    window = offset // 4
    corner = offset % 4
    row_pos = 2 * (window // half_w) + corner // 2
    col_pos = 2 * (window % half_w) + corner % 2
    return (row_pos.astype(jnp.float32), col_pos.astype(jnp.float32), areas, starts)


def rope_tables(row_pos, col_pos, head_dim):
    quarter = head_dim // 4
    lane = jnp.arange(LANES, dtype=jnp.int32)
    theta = 100.0 ** (-(lane % quarter).astype(jnp.float32) / quarter)
    part = lane // quarter
    pos = jnp.where(part[None, :] < 2, row_pos[:, None], col_pos[:, None])
    angles = pos * theta[None, :]
    cosine = jnp.cos(angles)
    sine = jnp.sin(angles)
    first = (part == 0) | (part == 2)
    second = (part == 1) | (part == 3)
    return (
        cosine,
        jnp.where(first[None, :], -sine, 0.0),
        jnp.where(second[None, :], sine, 0.0),
    )


def send_rows(proj_bf, starts, areas, owner_row, device_count):
    merged_rows = proj_bf.shape[0]
    wrap_count = (CAP + device_count - 1) // device_count
    dest_ids = jnp.arange(device_count, dtype=jnp.int32)[:, None, None]
    wrap_ids = jnp.arange(wrap_count, dtype=jnp.int32)[None, None, :]
    owner_here = owner_row[None, :, None]
    row_within = wrap_ids * device_count + (dest_ids - owner_here) % device_count
    row_total = (areas // 4)[None, :, None]
    first_row = (starts // 4)[None, :, None]
    picked = jnp.where(row_within < row_total, first_row + row_within, merged_rows)
    padded = jnp.concatenate([proj_bf, jnp.zeros((1, proj_bf.shape[1]), proj_bf.dtype)], axis=0)
    return padded[picked]


class Place:
    def __init__(self):
        me = lax.axis_index("dp")
        self.core = me % 2
        self.x = (me // 2) % 2
        self.y = (me // 4) % 2
        self.z = me // 8

    def line(self, r):
        z = self.z
        return (z, z + 1 - 2 * (z % 2), z + 2 - 4 * (z // 2), 3 - z)[r]

    def column(self, r, s):
        odd = (self.z + r) % 2
        x, y = self.x, self.y
        if s == 0:
            return y, x
        if s == 1:
            return y + odd * (1 - 2 * y), x + (1 - odd) * (1 - 2 * x)
        if s == 2:
            return y + (1 - odd) * (1 - 2 * y), x + odd * (1 - 2 * x)
        return 1 - y, 1 - x

    def chip(self, r, s):
        y, x = self.column(r, s)
        return (self.line(r) * 2 + y) * 2 + x

    def line_peer(self, r):
        return ((self.line(r) * 2 + self.y) * 2 + self.x) * 2 + self.core

    def side_peer(self, r, s):
        y, x = self.column(r, s)
        return ((self.z * 2 + y) * 2 + x) * 2 + self.core

    def twin(self):
        return ((self.z * 2 + self.y) * 2 + self.x) * 2 + 1 - self.core

    def greet(self):
        barrier = pltpu.get_barrier_semaphore()
        peers = [self.line_peer(r) for r in (1, 2, 3)]
        peers += [self.side_peer(0, 1), self.side_peer(0, 2), self.twin()]
        for peer in peers:
            pl.semaphore_signal(barrier, inc=1, device_id=(peer,), device_id_type=MESH)
        pl.semaphore_wait(barrier, len(peers))


class Gather:
    def __init__(self, place, src, dst_of, sems, at):
        self.place, self.src, self.dst_of = place, src, dst_of
        self.send, self.recv, self.twin_send, self.twin_recv, self.local = sems
        self.at = at
        self.ici = {}
        self.started = []

    def dst(self, r, s):
        return self.dst_of(self.place.chip(r, s))

    def remote(self, src, dst, send_sem, recv_sem, peer):
        copy = pltpu.make_async_remote_copy(
            src_ref=src,
            dst_ref=dst,
            send_sem=send_sem,
            recv_sem=recv_sem,
            device_id=(peer,),
            device_id_type=MESH,
        )
        copy.start()
        self.started.append(copy)
        return copy

    def over_links(self, src, unit, arrives, peer):
        n = self.at * 16 + arrives[0] * 4 + arrives[1]
        self.ici[arrives] = self.remote(
            src, self.dst(*unit), self.send.at[n], self.recv.at[n], peer
        )

    def to_twin(self, src, r, s):
        n = self.at * 16 + r * 4 + s
        self.twins.append(
            self.remote(
                src,
                self.dst(r, s),
                self.twin_send.at[n],
                self.twin_recv.at[n],
                self.place.twin(),
            )
        )

    def start(self):
        self.twins = []
        for r in (1, 2, 3):
            self.over_links(self.src, (0, 0), (r, 0), self.place.line_peer(r))
        self.spread(0)
        self.own = pltpu.make_async_copy(self.src, self.dst(0, 0), self.local.at[self.at])
        self.own.start()

    def spread(self, r):
        src = self.src if r == 0 else self.dst(r, 0)
        self.over_links(src, (r, 0), (r, 1), self.place.side_peer(r, 1))
        self.over_links(src, (r, 0), (r, 2), self.place.side_peer(r, 2))
        self.to_twin(src, r, 0)

    def second(self):
        for r in (1, 2, 3):
            self.ici[(r, 0)].wait_recv()
            self.spread(r)

    def third(self):
        for r in range(4):
            self.ici[(r, 1)].wait_recv()
            src = self.dst(r, 1)
            self.over_links(src, (r, 1), (r, 3), self.place.side_peer(r, 2))
            self.to_twin(src, r, 1)

    def fourth(self):
        for s in (2, 3):
            for r in range(4):
                self.ici[(r, s)].wait_recv()
                self.to_twin(self.dst(r, s), r, s)

    def finish(self):
        for copy in self.twins:
            copy.wait_recv()
        for copy in self.started:
            copy.wait_send()
        self.own.wait()


def gather_sems(chunks):
    return [pltpu.SemaphoreType.DMA((chunks * 16,))] * 4 + [pltpu.SemaphoreType.DMA((chunks,))]


def run_gathers(gathers, work):
    count = len(gathers)
    for step in range(count + 4):
        if step < count:
            gathers[step].start()
        work(step)
        if 0 <= step - 1 < count:
            gathers[step - 1].second()
        if 0 <= step - 2 < count:
            gathers[step - 2].third()
        if 0 <= step - 3 < count:
            gathers[step - 3].fourth()
        if 0 <= step - 4 < count:
            gathers[step - 4].finish()


def attend_kernel(
    q_chunks,
    p_chunks,
    scale,
    patches_ref,
    gain_ref,
    cos_ref,
    sin_a_ref,
    sin_b_ref,
    seg_col_ref,
    seg_row_ref,
    mask_row_ref,
    wq_ref,
    wo_ref,
    wp_ref,
    att_ref,
    top_ref,
    wq_all,
    wo_all,
    wp_all,
    wq_buf,
    q_buf,
    k_buf,
    v_buf,
    load_sem,
    *sems,
):
    place = Place()
    place.greet()
    depth, wq_cols = wq_ref.shape
    gathers = []
    wide = wq_cols // q_chunks
    for q in range(q_chunks):
        cols = slice(q * wide, (q + 1) * wide)

        def dst_of(chip, cols=cols):
            rows = pl.ds(pl.multiple_of(chip * depth, 8), depth)
            return wq_all.at[place.core, rows, cols]

        gathers.append(Gather(place, wq_ref.at[:, cols], dst_of, sems, len(gathers)))
    gathers.append(
        Gather(place, wo_ref, lambda chip: wo_all.at[place.core, chip], sems, len(gathers))
    )
    wide = wp_ref.shape[1] // p_chunks
    for q in range(p_chunks):
        cols = slice(q * wide, (q + 1) * wide)

        def dst_of(chip, cols=cols):
            return wp_all.at[chip, place.core, :, cols]

        gathers.append(Gather(place, wp_ref.at[:, cols], dst_of, sems, len(gathers)))
    tokens, width = patches_ref.shape
    block = 256
    half = HEADS // 2
    quarter = 26

    def project(i, carry):
        rows = pl.ds(pl.multiple_of(i * block, block), block)
        tokens_f = patches_ref[rows, :].astype(jnp.float32)
        centered = tokens_f - jnp.mean(tokens_f, axis=1, keepdims=True)
        var = jnp.mean(centered * centered, axis=1, keepdims=True)
        normed = (centered * lax.rsqrt(var + 1e-06) * gain_ref[...]).astype(jnp.bfloat16)
        cosine, sin_a, sin_b = cos_ref[rows, :], sin_a_ref[rows, :], sin_b_ref[rows, :]
        for part in range(2):
            mixed = jnp.dot(normed, wq_buf[part], preferred_element_type=jnp.float32)
            for kind, buf in ((0, q_buf), (1, k_buf), (2, v_buf)):
                for h in range(half):
                    at = (kind * half + h) * LANES
                    val = mixed[:, at : at + LANES]
                    if kind < 2:
                        val = (
                            val * cosine
                            + pltpu.roll(val, LANES - quarter, 1) * sin_a
                            + pltpu.roll(val, quarter, 1) * sin_b
                        )
                    out = (part * half + h) * LANES
                    buf[rows, out : out + LANES] = val.astype(jnp.bfloat16)
        return carry

    def one_block(i, carry):
        rows = pl.ds(pl.multiple_of(i * block, block), block)
        seg_q = seg_col_ref[rows, :]
        query_idx = i * block + lax.broadcasted_iota(jnp.int32, (block, tokens), 0)
        key_idx = lax.broadcasted_iota(jnp.int32, (block, tokens), 1)
        allowed = (seg_q == seg_row_ref[...]) & (
            (mask_row_ref[...] == 1) | (query_idx == key_idx)
        )
        bias = jnp.where(allowed, 0.0, -1e30)
        best = jnp.full((block, 1), -1e30, jnp.float32)
        for h in range(HEADS):
            lanes = slice(h * LANES, (h + 1) * LANES)
            scores = lax.dot_general(
                q_buf[rows, lanes],
                k_buf[:, lanes],
                (((1,), (1,)), ((), ())),
                preferred_element_type=jnp.float32,
            )
            scores = scores * scale + bias
            top = jnp.max(scores, axis=1, keepdims=True)
            best = jnp.maximum(best, top)
            expo = jnp.exp(scores - top)
            total = jnp.sum(expo, axis=1, keepdims=True)
            got = jnp.dot(
                expo.astype(jnp.bfloat16), v_buf[:, lanes], preferred_element_type=jnp.float32
            )
            att_ref[rows, lanes] = (got / total).astype(jnp.bfloat16)
        top_ref[rows, :] = jnp.broadcast_to(best, (block, LANES))
        return carry

    blocks = tokens // block
    loaded = q_chunks + 4

    def work(step):
        if step == loaded:
            load = pltpu.make_async_copy(wq_all, wq_buf, load_sem)
            load.start()
            load.wait()
            project(0, 0)
        elif step == loaded + 1:
            project(1, 0)
        elif step == loaded + 2:
            lax.fori_loop(2, blocks, project, 0)
        elif loaded + 3 <= step < loaded + 5:
            one_block(step - loaded - 3, 0)
        elif step == loaded + 5:
            lax.fori_loop(2, blocks, one_block, 0)

    run_gathers(gathers, work)


def attend_and_gather(patches, gain, tables, seg, mask, wq_block, wo_block, w_proj, head_dim):
    tokens, width = patches.shape
    q_chunks, p_chunks = 4, 8
    wide = HEADS * LANES
    vmem = pl.BlockSpec(memory_space=pltpu.VMEM)
    hbm = pl.BlockSpec(memory_space=pl.ANY)
    wq_shape = (2, width, wq_block.shape[1])
    return pl.pallas_call(
        functools.partial(attend_kernel, q_chunks, p_chunks, head_dim ** (-0.5)),
        out_shape=(
            jax.ShapeDtypeStruct((tokens, wide), jnp.bfloat16),
            jax.ShapeDtypeStruct((tokens, LANES), jnp.float32),
            jax.ShapeDtypeStruct(wq_shape, jnp.bfloat16),
            jax.ShapeDtypeStruct((2, 16) + wo_block.shape, jnp.bfloat16),
            jax.ShapeDtypeStruct((16, 2) + w_proj.shape, jnp.bfloat16),
        ),
        in_specs=[vmem] * 8 + [hbm] * 3,
        out_specs=(vmem, vmem, hbm, hbm, hbm),
        scratch_shapes=[pltpu.VMEM(wq_shape, jnp.bfloat16)]
        + [pltpu.VMEM((tokens, wide), jnp.bfloat16)] * 3
        + [pltpu.SemaphoreType.DMA]
        + gather_sems(q_chunks + 1 + p_chunks),
        compiler_params=pltpu.CompilerParams(
            collective_id=1, has_side_effects=True, vmem_limit_bytes=56 * 1024 * 1024
        ),
    )(
        patches,
        gain[None, :],
        *tables,
        seg[:, None],
        seg[None, :],
        mask[None, :],
        wq_block,
        wo_block,
        w_proj,
    )


def pair_blocks(w_qkv, w_out, head_dim):
    core = lax.axis_index("dp") % 2
    rows = w_qkv.shape[0]
    half = HEADS // 2
    pad = LANES - head_dim
    mine = jnp.concatenate([w_qkv, w_out.T], axis=1)
    twin = [(i, i + 1 - 2 * (i % 2)) for i in range(lax.axis_size("dp"))]
    parts = mine.reshape(rows, 4, 2, half, head_dim)
    keep = jnp.where(core == 0, parts[:, :, 0], parts[:, :, 1])
    give = jnp.where(core == 0, parts[:, :, 1], parts[:, :, 0])
    got = lax.ppermute(give.reshape(rows, -1), "dp", twin).reshape(keep.shape)
    both = jnp.concatenate(
        [jnp.where(core == 0, keep, got), jnp.where(core == 0, got, keep)], axis=0
    )
    both = jnp.pad(both, ((0, 0), (0, 0), (0, 0), (0, pad))).reshape(2 * rows, 4, half * LANES)
    return both[:, :3].reshape(2 * rows, 3 * half * LANES), both[:, 3]


def plain_gathers(patches, ln_gain, tables, seg_ids, patch_mask, w_qkv, w_out, w_proj):
    tok_count = patches.shape[0]
    tokens_f = patches.astype(jnp.float32)
    mean_row = jnp.mean(tokens_f, axis=-1, keepdims=True)
    centered = tokens_f - mean_row
    var_row = jnp.mean(centered * centered, axis=-1, keepdims=True)
    normed = (centered * lax.rsqrt(var_row + 1e-06) * ln_gain).astype(jnp.bfloat16)
    hidden_w = w_out.shape[0]
    head_dim = hidden_w // HEADS
    quarter = head_dim // 4
    mixed = jnp.dot(
        normed, lax.all_gather(w_qkv, "dp", axis=0, tiled=True), preferred_element_type=jnp.float32
    )
    shape_three = (tok_count, HEADS, head_dim)
    cosine, sin_a, sin_b = [t[:, None, :head_dim] for t in tables]

    def rotate(val):
        return (
            val * cosine
            + jnp.roll(val, -quarter, axis=2) * sin_a
            + jnp.roll(val, quarter, axis=2) * sin_b
        ).astype(jnp.bfloat16)

    queries = rotate(mixed[:, :hidden_w].reshape(shape_three))
    key_rows = rotate(mixed[:, hidden_w : 2 * hidden_w].reshape(shape_three))
    values = mixed[:, 2 * hidden_w :].reshape(shape_three).astype(jnp.bfloat16)
    scores = jnp.einsum("qhd,khd->hqk", queries, key_rows, preferred_element_type=jnp.float32)
    idx = jnp.arange(tok_count, dtype=jnp.int32)
    allowed = (seg_ids[:, None] == seg_ids[None, :]) & (
        (patch_mask[None, :] == 1) | (idx[:, None] == idx[None, :])
    )
    masked = jnp.where(allowed[None], scores * head_dim ** (-0.5), -1e30)
    weights = jax.nn.softmax(masked, axis=-1).astype(jnp.bfloat16)
    attended = jnp.einsum("hqk,khd->qhd", weights, values, preferred_element_type=jnp.float32)
    attended = attended.astype(jnp.bfloat16).reshape(tok_count, hidden_w)
    out_term = jnp.dot(
        attended,
        lax.all_gather(w_out, "dp", axis=1, tiled=True),
        preferred_element_type=jnp.float32,
    )
    return out_term, jnp.max(masked, axis=(0, 2)), lax.all_gather(w_proj, "dp", axis=0, tiled=True)


def chip_gathers(patches, ln_gain, tables, seg_ids, patch_mask, w_qkv, w_out, w_proj):
    head_dim = w_out.shape[0] // HEADS
    wq_block, wo_block = pair_blocks(w_qkv, w_out, head_dim)
    att, top, _, wo, wp = attend_and_gather(
        patches, ln_gain, tables, seg_ids, patch_mask, wq_block, wo_block, w_proj, head_dim
    )
    wo = wo.reshape(2, -1, wo_block.shape[1])
    span = wo.shape[2]
    dims = (((1,), (1,)), ((), ()))
    out_term = lax.dot_general(
        att[:, :span], wo[0], dims, preferred_element_type=jnp.float32
    ) + lax.dot_general(att[:, span:], wo[1], dims, preferred_element_type=jnp.float32)
    return out_term, top[:, 0], wp.reshape(-1, w_proj.shape[1])


def on_device(patches, ln_gain, w_qkv, w_out, w_proj, seg_ids, patch_mask, grid_hw, owners):
    tok_count, width_in = patches.shape
    head_dim = w_out.shape[0] // HEADS
    image_count = grid_hw.shape[0]
    proj_w = w_proj.shape[1]
    devices = lax.axis_size("dp")
    tokens_f = patches.astype(jnp.float32)
    row_pos, col_pos, areas, starts = token_places(seg_ids, grid_hw)
    tables = rope_tables(row_pos, col_pos, head_dim)
    image_ids = jnp.arange(image_count, dtype=jnp.int32)
    path = chip_gathers if devices == 32 else plain_gathers
    out_term, row_top, wp = path(
        patches, ln_gain, tables, seg_ids, patch_mask, w_qkv, w_out, w_proj
    )
    member_q = seg_ids[:, None] == image_ids[None, :]
    top_logit = jnp.max(jnp.where(member_q, row_top[:, None], -1e30), axis=0)
    residual = (tokens_f + out_term).astype(jnp.bfloat16)
    merged = residual.reshape(tok_count // 4, 4 * width_in)
    projected = jnp.dot(merged, wp, preferred_element_type=jnp.float32)
    proj_bf = projected.astype(jnp.bfloat16)
    merged_seg = seg_ids.reshape(-1, 4)[:, 0]
    member_m = merged_seg[:, None] == image_ids[None, :]
    squares = jnp.sum(projected * projected, axis=1)
    totals = jnp.sum(jnp.where(member_m, squares[:, None], 0.0), axis=0)
    image_rms = jnp.sqrt(totals / (areas // 4 * proj_w).astype(jnp.float32))
    sent = send_rows(proj_bf, starts, areas, owners, devices)
    arrived = lax.all_to_all(sent, "dp", split_axis=0, concat_axis=0, tiled=True)
    return (arrived.reshape(-1, proj_w), image_rms, top_logit)


def solution(mesh):
    return jax.shard_map(
        on_device,
        mesh=mesh,
        in_specs=(
            P("dp", None),
            P(),
            P("dp", None),
            P(None, "dp"),
            P("dp", None),
            P("dp"),
            P("dp"),
            P("dp", None),
            P("dp"),
        ),
        out_specs=(P("dp", None), P("dp"), P("dp")),
        check_vma=False,
    )
```
